128 devices in a mesh: modes: 32 (over y, z, x_lo), mesh: 4 (over x_hi, core).
Axes of the slice: x: 4 (x_hi: 2, x_lo: 2; x = x_hi * 2 + x_lo), y: 4, z: 4, core: 2. Of those that a mesh axis runs over, the one named last changes fastest.
Arguments:
- velocity: float32 [3, 64, 2, 12288], P(None, 'modes', None, 'mesh'), may hold values from -0.4 to 0.4
- blocks: float32 [96, 9, 128, 128], P('mesh'), may hold values from -0.09375 to 0.09375
- neighbours: int32 [96, 9], P('mesh'), may hold values from 0 to 95, as said below
- element_derivative: float32 [2, 16, 16], replicated, may hold values from -1.5 to 1.5
Outputs:
- advanced: float32 [3, 64, 2, 12288], P(None, 'modes', None, 'mesh')
The draws below stay inside these ranges and needn't reach their ends.
Inputs may be any that keep to these rules, and one draw needn't show every extreme that they name: neighbours[r, j] differs from r by at most 2; neighbours[r, 4] = r, and neighbours[r, 0] = r - 2, neighbours[r, 8] = r + 2 where these lie in range, else the nearest block row in range.
All inputs are finite; a program needn't handle non-finite values.
Results may differ from the reference program's by a relative error of at most 0.0003.
Values sent between devices are 32-bit elements; how exact they have to be, the bound alone decides.
No kernel may reach another device: no remote copies, remote signals or barrier semaphores. Data moves between devices by JAX's collectives and lax.ppermute only.
A program may use at most 192 MiB of HBM per device.

```python
import jax
import jax.numpy as jnp
from jax import lax

MODES = 64
BLK = 128
ELEM = 16
HW = 2
SWEEPS = 3
STEPS = 5
PLANE = 12288
NBLK = 96


def draw_neighbours(key, part):
    offsets = jax.random.randint(key, (NBLK, 9), -HW, HW + 1)
    slot_index = jnp.arange(9, dtype=jnp.int32)[None, :]
    offsets = jnp.where(slot_index == 0, -HW, jnp.where(slot_index == 4, 0, jnp.where(slot_index == 8, HW, offsets)))
    row_index = jnp.arange(NBLK, dtype=jnp.int32)[:, None]
    return jnp.clip(row_index + offsets, 0, NBLK - 1).astype(jnp.int32)


def steps_of(stream_key, extent, shards, low, high):
    factor_of = 1.0
    for position, blocks in shards:
        heights = jax.random.uniform(jax.random.fold_in(jax.random.fold_in(stream_key, 6), position), (blocks,), jnp.float32, low / len(shards), high / len(shards))
        factor_of = factor_of * jnp.repeat(jnp.exp(heights), extent[position] // blocks).reshape((-1,) + (1,) * (len(extent) - 1 - position))
    return factor_of


def gaussian(own_key, dims, deviation, bound, pieces=(), kind=jnp.bfloat16):
    gain = steps_of(own_key, dims, pieces, -0.22, 0.18) if pieces else 1.0
    result = jax.random.normal(own_key, dims, jnp.float32) * deviation * gain
    return jnp.minimum(jnp.maximum(result, -bound), bound).astype(kind)


def setup_inputs(seed: int = 0) -> dict:
    streams_of = jax.random.split(jax.random.key(seed), 5)
    velocity = gaussian(streams_of[0], (3, MODES, 2, PLANE), 0.0625, 0.4, ((1, 32), (3, 4)), jnp.float32)
    blocks = gaussian(streams_of[1], (NBLK, 9, BLK, BLK), (0.5 / (3 * BLK ** 0.5)), 0.09375, ((0, 4),), jnp.float32)
    neighbours = draw_neighbours(jax.random.fold_in(streams_of[4], 71), 0)
    element_derivative = gaussian(streams_of[3], (2, ELEM, ELEM), ELEM ** -0.5, 1.5, (), jnp.float32)
    return dict(velocity=velocity, blocks=blocks, neighbours=neighbours, element_derivative=element_derivative)


PRECISE = lax.Precision.HIGHEST
PRODUCT_PAIRS = ((0, 0), (0, 1), (0, 2), (1, 1), (1, 2), (2, 2))
VISCOSITY = 0.1
TIME_STEP = 0.2
HALF_WIDTH = 0.6
SPAN_WAVE = 1.0 / 16.0


def pair_slot(left_index, right_index):
    return PRODUCT_PAIRS.index((min(left_index, right_index), max(left_index, right_index)))


def tables(mode_count):
    points = 2 * mode_count
    z_index = jnp.arange(points, dtype=jnp.int32)[:, None]
    k_index = jnp.arange(mode_count, dtype=jnp.int32)[None, :]
    angles = (2.0 * jnp.pi / points) * ((z_index * k_index) % points).astype(jnp.float32)
    cosine = jnp.cos(angles)
    sine = jnp.sin(angles)
    weights = jnp.where(k_index == 0, 1.0, 2.0).astype(jnp.float32)
    inverse = jnp.stack([weights * cosine, -weights * sine], axis=2)
    forward = jnp.stack([cosine.T, -sine.T], axis=1) / points
    wave = jnp.arange(mode_count, dtype=jnp.float32) * SPAN_WAVE
    return inverse, forward, wave


def plane_derivative(values, matrix):
    full_shape = values.shape
    grouped = values.reshape(full_shape[:-1] + (full_shape[-1] // ELEM, ELEM))
    return jnp.einsum("ij,...ej->...ei", matrix, grouped, precision=PRECISE).reshape(full_shape)


def assemble(spectra, wave, element_derivative):
    terms = []
    for axis_index in range(3):
        along = spectra[pair_slot(axis_index, 2)]
        spanwise = jnp.stack([-wave[:, None] * along[:, 1], wave[:, None] * along[:, 0]], axis=1)
        planar = plane_derivative(spectra[pair_slot(axis_index, 0)], element_derivative[0])
        planar = planar + plane_derivative(spectra[pair_slot(axis_index, 1)], element_derivative[1])
        terms.append(spanwise + planar)
    return jnp.stack(terms)


def chebyshev(right_side, diagonal_shift, apply_coupling):
    sigma_ratio = diagonal_shift / HALF_WIDTH
    ratio_old = 1.0 / sigma_ratio
    solution = jnp.zeros_like(right_side)
    residual = right_side
    direction = right_side / diagonal_shift
    for sweep_index in range(SWEEPS):
        solution = solution + direction
        residual = residual - (diagonal_shift * direction + apply_coupling(direction))
        ratio_new = 1.0 / (2.0 * sigma_ratio - ratio_old)
        direction = ratio_new * ratio_old * direction + (2.0 * ratio_new / HALF_WIDTH) * residual
        ratio_old = ratio_new
    return solution + direction


def reference(velocity, blocks, neighbours, element_derivative):
    inverse, forward, wave = tables(MODES)
    diagonal_shift = (1.0 + VISCOSITY * wave * wave)[None, :, None, None]

    def apply_coupling(vector_field):
        full_shape = vector_field.shape
        rows = vector_field.reshape(-1, NBLK, BLK)
        total = jnp.zeros(rows.shape, jnp.float32)
        for slot_index in range(9):
            picked = rows[:, neighbours[:, slot_index], :]
            total = total + jnp.einsum("cnq,npq->cnp", picked, blocks[:, slot_index], precision=PRECISE)
        return total.reshape(full_shape)

    state = velocity
    for time_index in range(STEPS):
        physical = jnp.einsum("zkr,ckrp->czp", inverse, state, precision=PRECISE)
        products = jnp.stack([physical[a] * physical[b] for a, b in PRODUCT_PAIRS])
        spectra = jnp.einsum("krz,mzp->mkrp", forward, products, precision=PRECISE)
        forcing = assemble(spectra, wave, element_derivative)
        right_side = state - TIME_STEP * forcing
        state = chebyshev(right_side, diagonal_shift, apply_coupling)
    return state
```

```python
import jax
import jax.numpy as jnp
import numpy as np
from jax import lax
from jax.experimental import pallas as pl
from jax.experimental.pallas import tpu as pltpu
from jax.sharding import Mesh
from jax.sharding import PartitionSpec as P

ELEM = 16
HW = 2
SWEEPS = 3
STEPS = 5
BLK = 128
BAND = 2 * HW + 1

VISCOSITY = 0.1
TIME_STEP = 0.2
HALF_WIDTH = 0.6
SPAN_WAVE = 1.0 / 16.0

MODES = 64
POINTS = 2 * MODES
PAIRS = ((0, 0), (0, 1), (0, 2), (1, 1), (1, 2), (2, 2))
AXES = ("y", "z", "xl", "xh", "co")
TEAM = 8
OWN = 6
VEC = 48
EDGE = 2 * HW
WIN = 3 * OWN
ROWS = OWN + 2 * EDGE
LOCAL = 24

F32 = jnp.float32
BF16 = jnp.bfloat16


def device_of(y, z, xl, xh, co):
    return (((y * 4 + z) * 2 + xl) * 2 + xh) * 2 + co


def team_devices(rank):
    s, q = divmod(rank, 4)
    xh, co = divmod(s, 2)
    y = q if co == 0 else 3 - q
    return [device_of(y, z, xl, xh, co) for z in range(4) for xl in range(2)]


def shift_pairs(step):
    return [
        (a, b)
        for rank in range(16)
        if 0 <= rank + step < 16
        for a, b in zip(team_devices(rank), team_devices(rank + step))
    ]


def seam_pairs():
    pairs = []
    for rank in (3, 7, 11):
        for a, b in zip(team_devices(rank), team_devices(rank + 1)):
            pairs += [(a, b), (b, a)]
    return pairs


def split_np(x):
    hi = x.astype(BF16)
    lo = (x - hi.astype(np.float64)).astype(BF16)
    return hi, lo


def mode_rows():
    modes, parts = [], []
    for member in range(TEAM):
        for y in range(4):
            for m in range(2):
                for r in range(2):
                    modes.append(2 * (y * 8 + member) + m)
                    parts.append(r)
    return np.array(modes), np.array(parts)


def tables():
    modes, parts = mode_rows()
    z = np.arange(POINTS)
    angle = 2.0 * np.pi / POINTS * ((z[:, None] * modes[None, :]) % POINTS)
    cosine, sine = np.cos(angle), np.sin(angle)
    weight = np.where(modes == 0, 1.0, 2.0)
    inverse = np.where(parts == 0, cosine, -sine) * weight
    forward = (np.where(parts == 0, cosine, -sine) / POINTS).T
    wave = modes * SPAN_WAVE
    other = (np.where(parts == 0, -sine, cosine) / POINTS).T
    spanwise = np.where(parts == 0, -wave, wave)[:, None] * other
    both = -TIME_STEP * np.concatenate([forward, spanwise], axis=1)
    ihi, ilo = split_np(inverse)
    fhi, flo = split_np(both)
    return (
        np.concatenate([ihi, ihi, ilo], axis=1),
        np.concatenate([fhi, flo], axis=0),
    )


def solve_coefficients():
    shift = 1.0 + VISCOSITY * (np.arange(MODES) * SPAN_WAVE) ** 2
    sigma = shift / HALF_WIDTH
    old = 1.0 / sigma
    width = SWEEPS + 1
    residual = np.zeros((MODES, width))
    residual[:, 0] = 1.0
    direction = residual / shift[:, None]
    total = np.zeros((MODES, width))
    for _ in range(SWEEPS):
        total = total + direction
        moved = np.concatenate([np.zeros((MODES, 1)), direction[:, :-1]], axis=1)
        residual = residual - (shift[:, None] * direction + moved)
        new = 1.0 / (2.0 * sigma - old)
        direction = (new * old)[:, None] * direction + (2.0 * new / HALF_WIDTH)[:, None] * residual
        old = new
    total = total + direction
    modes, _ = mode_rows()
    out = np.zeros((TEAM, VEC, BLK), np.float32)
    for member in range(TEAM):
        for c in range(3):
            for i in range(16):
                out[member, c * 16 + i, :width] = total[modes[member * 16 + i]]
    return out


def split(x):
    hi = x.astype(BF16)
    return hi, (x - hi.astype(F32)).astype(BF16)


def full(shape):
    return pl.BlockSpec(shape, lambda *_: (0,) * len(shape))


def vmem(n):
    return [pl.BlockSpec(memory_space=pltpu.VMEM)] * n


LIMIT = pltpu.CompilerParams(vmem_limit_bytes=40 * 2**20)


def scatter_body(flip_ref, velocity_ref, out_ref):
    flip = flip_ref[0]
    out_ref[...] = jnp.zeros_like(out_ref)
    for q in range(4):
        y = q + flip * (3 - 2 * q)
        for j in range(OWN):
            lanes = slice((q * OWN + j) * BLK, (q * OWN + j + 1) * BLK)
            for c in range(3):
                for m in range(2):
                    row = (c * 2 + m) * 2
                    out_ref[y * TEAM + j, row : row + 2, :] = velocity_ref[c, m, :, lanes]


def scatter(flip, velocity):
    return pl.pallas_call(
        scatter_body,
        out_shape=jax.ShapeDtypeStruct((4 * TEAM, 16, BLK), F32),
        in_specs=[pl.BlockSpec(memory_space=pltpu.SMEM)] + vmem(1),
        out_specs=vmem(1)[0],
        compiler_params=LIMIT,
        name="scatter",
    )(flip, velocity)


def nonlinear_core(state, inverse_ref, derivative_ref, forward_ref):
    hi, lo = split(state)
    physical = jnp.dot(inverse_ref[...], jnp.concatenate([hi, lo, hi], axis=0), preferred_element_type=F32)
    field = [physical[:, c * BLK : (c + 1) * BLK] for c in range(3)]
    products = {pair: field[pair[0]] * field[pair[1]] for pair in PAIRS}

    def product(a, b):
        return products[(min(a, b), max(a, b))]

    left = jnp.concatenate([jnp.concatenate([product(a, 0), product(a, 1)], axis=1) for a in range(3)], axis=0)
    left_hi, left_lo = split(left)
    der_hi, der_lo = split(derivative_ref[...])
    planar = jnp.dot(
        jnp.concatenate([left_hi, left_lo], axis=0),
        jnp.concatenate([der_hi, der_lo], axis=1),
        preferred_element_type=F32,
    )
    rows = 3 * POINTS
    planar = planar[:rows, :BLK] + planar[:rows, BLK:] + planar[rows:, :BLK]
    right = jnp.concatenate(
        [jnp.concatenate([planar[a * POINTS : (a + 1) * POINTS], product(a, 2)], axis=0) for a in range(3)], axis=1
    )
    right_hi, right_lo = split(right)
    first = jnp.dot(forward_ref[...], right_hi, preferred_element_type=F32)
    second = jnp.dot(forward_ref[:POINTS, :], right_lo, preferred_element_type=F32)
    return state + (first[:POINTS] + first[POINTS:] + second)


def store_chunks(right_side, out_ref):
    for j in range(TEAM):
        for c in range(3):
            out_ref[j, c * 16 : (c + 1) * 16, :] = right_side[j * 16 : (j + 1) * 16, c * BLK : (c + 1) * BLK]


def first_body(chunks_ref, inverse_ref, derivative_ref, forward_ref, out_ref, state_ref):
    for device in range(4 * TEAM):
        y, member = divmod(device, TEAM)
        row = member * 16 + y * 4
        for c in range(3):
            state_ref[row : row + 4, c * BLK : (c + 1) * BLK] = chunks_ref[device, c * 4 : (c + 1) * 4, :]
    store_chunks(nonlinear_core(state_ref[...], inverse_ref, derivative_ref, forward_ref), out_ref)


def later_body(chunks_ref, inverse_ref, derivative_ref, forward_ref, out_ref):
    state = jnp.concatenate(
        [
            jnp.concatenate([chunks_ref[j, c * 16 : (c + 1) * 16, :] for j in range(TEAM)], axis=0)
            for c in range(3)
        ],
        axis=1,
    )
    store_chunks(nonlinear_core(state, inverse_ref, derivative_ref, forward_ref), out_ref)


def nonlinear(chunks, inverse, derivative, forward, first):
    return pl.pallas_call(
        first_body if first else later_body,
        out_shape=jax.ShapeDtypeStruct((TEAM, VEC, BLK), F32),
        in_specs=vmem(4),
        out_specs=vmem(1)[0],
        scratch_shapes=[pltpu.VMEM((POINTS, 3 * BLK), F32)] if first else [],
        compiler_params=LIMIT,
        name="nonlinear",
    )(chunks, inverse, derivative, forward)


def band_rows(near_ref, blocks_ref, row, centre, acc_ref):
    acc_ref[...] = jnp.zeros_like(acc_ref)
    for slot in range(9):
        offset = near_ref[row * 9 + slot] - centre + HW
        acc_ref[offset] += blocks_ref[0, slot]


def edge_body(near_ref, info_ref, blocks_ref, out_ref, acc_ref):
    row = info_ref[1] + pl.program_id(0)
    band_rows(near_ref, blocks_ref, row, info_ref[0] + row, acc_ref)
    out_ref[0] = acc_ref[...]


def edge_band(near, info, blocks):
    return pl.pallas_call(
        edge_body,
        out_shape=jax.ShapeDtypeStruct((EDGE, BAND, BLK, BLK), F32),
        grid_spec=pltpu.PrefetchScalarGridSpec(
            num_scalar_prefetch=2,
            grid=(EDGE,),
            in_specs=[pl.BlockSpec((1, 9, BLK, BLK), lambda i, near, info: (info[1] + i, 0, 0, 0))],
            out_specs=pl.BlockSpec((1, BAND, BLK, BLK), lambda i, near, info: (i, 0, 0, 0)),
            scratch_shapes=[pltpu.VMEM((BAND, BLK, BLK), F32)],
        ),
        compiler_params=LIMIT,
        name="edge_band",
    )(near, info, blocks)


def weight_body(near_ref, info_ref, blocks_ref, edge_ref, out_ref, acc_ref):
    row = info_ref[2] + pl.program_id(0)
    inside = jnp.logical_and(row >= 0, row < LOCAL)

    @pl.when(inside)
    def _():
        band_rows(near_ref, blocks_ref, row, info_ref[0] + row, acc_ref)

    @pl.when(jnp.logical_not(inside))
    def _():
        acc_ref[...] = edge_ref[0]

    for offset in range(BAND):
        hi, lo = split(acc_ref[offset].T)
        out_ref[0, offset * BLK : (offset + 1) * BLK, :BLK] = hi
        out_ref[0, offset * BLK : (offset + 1) * BLK, BLK:] = lo


def weights_of(near, info, blocks, edge):
    return pl.pallas_call(
        weight_body,
        out_shape=jax.ShapeDtypeStruct((ROWS, BAND * BLK, 2 * BLK), BF16),
        grid_spec=pltpu.PrefetchScalarGridSpec(
            num_scalar_prefetch=2,
            grid=(ROWS,),
            in_specs=[
                pl.BlockSpec(
                    (1, 9, BLK, BLK), lambda i, near, info: (jnp.clip(info[2] + i, 0, LOCAL - 1), 0, 0, 0)
                ),
                pl.BlockSpec(
                    (1, BAND, BLK, BLK),
                    lambda i, near, info: (
                        jnp.where(
                            info[2] + i < 0, info[2] + i + EDGE, jnp.clip(info[2] + i - LOCAL, 0, EDGE - 1)
                        ),
                        0,
                        0,
                        0,
                    ),
                ),
            ],
            out_specs=pl.BlockSpec((1, BAND * BLK, 2 * BLK), lambda i, near, info: (i, 0, 0)),
            scratch_shapes=[pltpu.VMEM((BAND, BLK, BLK), F32)],
        ),
        compiler_params=LIMIT,
        name="weights",
    )(near, info, blocks, edge)


def solve_values(own_ref, left_ref, right_ref, weight_ref, coef_ref):
    def window(w):
        if w < OWN:
            return left_ref[w]
        return own_ref[w - OWN] if w < 2 * OWN else right_ref[w - 2 * OWN]

    def stacked(x):
        return jnp.concatenate(split(x), axis=0)

    def apply(parts, rows):
        out = {}
        for w in rows:
            lhs = jnp.concatenate([parts[w + o] for o in range(-HW, HW + 1)], axis=1)
            both = jnp.dot(lhs, weight_ref[w - HW], preferred_element_type=F32)
            out[w] = both[:VEC, :BLK] + both[:VEC, BLK:] + both[VEC:, :BLK]
        return out

    one = apply({w: stacked(window(w)) for w in range(WIN)}, range(HW, WIN - HW))
    two = apply({w: stacked(x) for w, x in one.items()}, range(2 * HW, WIN - 2 * HW))
    three = apply({w: stacked(x) for w, x in two.items()}, range(3 * HW, WIN - 3 * HW))
    coef = [coef_ref[:, i : i + 1] for i in range(SWEEPS + 1)]
    return [
        coef[0] * window(w) + coef[1] * one[w] + coef[2] * two[w] + coef[3] * three[w]
        for w in range(OWN, 2 * OWN)
    ]


def solve_body(own_ref, left_ref, right_ref, weight_ref, coef_ref, out_ref):
    for j, x in enumerate(solve_values(own_ref, left_ref, right_ref, weight_ref, coef_ref)):
        out_ref[j] = x
    out_ref[OWN:] = jnp.zeros((TEAM - OWN, VEC, BLK), F32)


def last_body(own_ref, left_ref, right_ref, weight_ref, coef_ref, out_ref):
    for j, x in enumerate(solve_values(own_ref, left_ref, right_ref, weight_ref, coef_ref)):
        for y in range(4):
            for c in range(3):
                out_ref[y, j, c * 4 : (c + 1) * 4, :] = x[c * 16 + y * 4 : c * 16 + y * 4 + 4]
            out_ref[y, j, 12:, :] = jnp.zeros((4, BLK), F32)


def solve(own, left, right, weights, coef, last):
    shape = (4, OWN, 16, BLK) if last else (TEAM, VEC, BLK)
    return pl.pallas_call(
        last_body if last else solve_body,
        out_shape=jax.ShapeDtypeStruct(shape, F32),
        in_specs=vmem(5),
        out_specs=vmem(1)[0],
        compiler_params=LIMIT,
        name="solve",
    )(own, left, right, weights, coef)


def gather_body(flip_ref, chunks_ref, out_ref):
    flip = flip_ref[0]
    for q in range(4):
        y = q + flip * (3 - 2 * q)
        for j in range(OWN):
            lanes = slice((q * OWN + j) * BLK, (q * OWN + j + 1) * BLK)
            for c in range(3):
                for m in range(2):
                    row = (c * 2 + m) * 2
                    out_ref[c, m, :, lanes] = chunks_ref[y, j, row : row + 2, :]


def gather(flip, chunks):
    return pl.pallas_call(
        gather_body,
        out_shape=jax.ShapeDtypeStruct((3, 2, 2, LOCAL * BLK), F32),
        in_specs=[pl.BlockSpec(memory_space=pltpu.SMEM)] + vmem(1),
        out_specs=vmem(1)[0],
        compiler_params=LIMIT,
        name="gather",
    )(flip, chunks)


def on_device(velocity, blocks, neighbours, element_derivative):
    y, z, xl, xh, co = (lax.axis_index(axis) for axis in AXES)
    part = xh * 2 + co
    q = y + co * (3 - 2 * y)
    flip = co.reshape(1)
    info = jnp.stack([part * LOCAL, jnp.where(q < 2, 0, LOCAL - EDGE), q * OWN - EDGE]).astype(jnp.int32)
    near = neighbours.reshape(-1)
    inverse_np, forward_np = tables()
    inverse, forward = jnp.asarray(inverse_np), jnp.asarray(forward_np)
    coef = lax.dynamic_index_in_dim(jnp.asarray(solve_coefficients()), z * 2 + xl, 0, keepdims=False)
    count = BLK // ELEM
    eye = jnp.eye(count, dtype=F32)
    derivative = (
        eye[None, :, None, :, None] * element_derivative.transpose(0, 2, 1)[:, None, :, None, :]
    ).reshape(2 * BLK, BLK)

    edge = lax.ppermute(edge_band(near, info, blocks), AXES, seam_pairs())
    chunks = lax.all_to_all(scatter(flip, velocity), ("y", "z", "xl"), 0, 0, tiled=True)
    weights = None
    for step in range(STEPS):
        right_side = nonlinear(chunks, inverse, derivative, forward, step == 0)
        own = lax.all_to_all(right_side, ("z", "xl"), 0, 0, tiled=True)
        if weights is None:
            weights = weights_of(near, info, blocks, edge)
        mine = own[:OWN]
        left = lax.ppermute(mine, AXES, shift_pairs(1))
        right = lax.ppermute(mine, AXES, shift_pairs(-1))
        last = step == STEPS - 1
        chunks = solve(own, left, right, weights, coef, last)
        if not last:
            chunks = lax.all_to_all(chunks, ("z", "xl"), 0, 0, tiled=True)
    return gather(flip, lax.all_to_all(chunks, ("y",), 0, 0, tiled=True))


def solution(mesh):
    fine = Mesh(mesh.devices.reshape(4, 4, 2, 2, 2), AXES)
    field = P(None, ("y", "z", "xl"), None, ("xh", "co"))
    in_specs = (field, P(("xh", "co"), None, None, None), P(("xh", "co"), None), P())
    return jax.shard_map(on_device, mesh=fine, in_specs=in_specs, out_specs=field, check_vma=False)
```

```python
import jax
import jax.numpy as jnp
import numpy as np
from jax import lax
from jax.experimental import pallas as pl
from jax.experimental.pallas import tpu as pltpu
from jax.sharding import Mesh
from jax.sharding import PartitionSpec as P

ELEM = 16
HW = 2
SWEEPS = 3
STEPS = 5
BLK = 128
BAND = 2 * HW + 1

VISCOSITY = 0.1
TIME_STEP = 0.2
HALF_WIDTH = 0.6
SPAN_WAVE = 1.0 / 16.0

MODES = 64
POINTS = 2 * MODES
PAIRS = ((0, 0), (0, 1), (0, 2), (1, 1), (1, 2), (2, 2))
AXES = ("y", "z", "xl", "xh", "co")
TEAM = 8
OWN = 6
VEC = 48
EDGE = 2 * HW
WIN = 3 * OWN
ROWS = OWN + 2 * EDGE
LOCAL = 24

F32 = jnp.float32
BF16 = jnp.bfloat16


def device_of(y, z, xl, xh, co):
    return (((y * 4 + z) * 2 + xl) * 2 + xh) * 2 + co


def team_devices(rank):
    s, q = divmod(rank, 4)
    xh, co = divmod(s, 2)
    y = q if co == 0 else 3 - q
    return [device_of(y, z, xl, xh, co) for z in range(4) for xl in range(2)]


def swap_pairs(first):
    pairs = []
    for rank in range(first, 15, 2):
        for a, b in zip(team_devices(rank), team_devices(rank + 1)):
            pairs += [(a, b), (b, a)]
    return pairs


def seam_pairs():
    pairs = []
    for rank in (3, 7, 11):
        for i, a in enumerate(team_devices(rank)):
            b = team_devices(rank + 1)[i ^ 1 if rank == 7 else i]
            pairs += [(a, b), (b, a)]
    return pairs


def split_np(x):
    hi = x.astype(BF16)
    lo = (x - hi.astype(np.float64)).astype(BF16)
    return hi, lo


def mode_rows():
    modes, parts = [], []
    for member in range(TEAM):
        for y in range(4):
            for m in range(2):
                for r in range(2):
                    modes.append(2 * (y * 8 + member) + m)
                    parts.append(r)
    return np.array(modes), np.array(parts)


def tables():
    modes, parts = mode_rows()
    z = np.arange(POINTS)
    angle = 2.0 * np.pi / POINTS * ((z[:, None] * modes[None, :]) % POINTS)
    cosine, sine = np.cos(angle), np.sin(angle)
    weight = np.where(modes == 0, 1.0, 2.0)
    inverse = np.where(parts == 0, cosine, -sine) * weight
    forward = (np.where(parts == 0, cosine, -sine) / POINTS).T
    wave = modes * SPAN_WAVE
    other = (np.where(parts == 0, -sine, cosine) / POINTS).T
    spanwise = np.where(parts == 0, -wave, wave)[:, None] * other
    both = -TIME_STEP * np.concatenate([forward, spanwise], axis=1)
    ihi, ilo = split_np(inverse)
    fhi, flo = split_np(both)
    return (
        np.concatenate([ihi, ihi, ilo], axis=1),
        np.concatenate([fhi, flo], axis=0),
    )


def solve_coefficients():
    shift = 1.0 + VISCOSITY * (np.arange(MODES) * SPAN_WAVE) ** 2
    sigma = shift / HALF_WIDTH
    old = 1.0 / sigma
    width = SWEEPS + 1
    residual = np.zeros((MODES, width))
    residual[:, 0] = 1.0
    direction = residual / shift[:, None]
    total = np.zeros((MODES, width))
    for _ in range(SWEEPS):
        total = total + direction
        moved = np.concatenate([np.zeros((MODES, 1)), direction[:, :-1]], axis=1)
        residual = residual - (shift[:, None] * direction + moved)
        new = 1.0 / (2.0 * sigma - old)
        direction = (new * old)[:, None] * direction + (2.0 * new / HALF_WIDTH)[:, None] * residual
        old = new
    total = total + direction
    modes, _ = mode_rows()
    out = np.zeros((TEAM, VEC, BLK), np.float32)
    for member in range(TEAM):
        for c in range(3):
            for i in range(16):
                out[member, c * 16 + i, :width] = total[modes[member * 16 + i]]
    return out


def split(x):
    hi = x.astype(BF16)
    return hi, (x - hi.astype(F32)).astype(BF16)


def full(shape):
    return pl.BlockSpec(shape, lambda *_: (0,) * len(shape))


def vmem(n):
    return [pl.BlockSpec(memory_space=pltpu.VMEM)] * n


LIMIT = pltpu.CompilerParams(vmem_limit_bytes=12 * 2**20)
LARGE = pltpu.CompilerParams(vmem_limit_bytes=40 * 2**20)


def cost(flops, transferred):
    return pl.CostEstimate(flops=flops, bytes_accessed=transferred, transcendentals=0)


def scatter_body(flip_ref, velocity_ref, out_ref, done_ref):
    flip = flip_ref[0]
    done_ref[...] = jnp.zeros_like(done_ref)
    out_ref[...] = jnp.zeros_like(out_ref)
    for q in range(4):
        y = q + flip * (3 - 2 * q)
        for j in range(OWN):
            lanes = slice((q * OWN + j) * BLK, (q * OWN + j + 1) * BLK)
            for c in range(3):
                for m in range(2):
                    row = (c * 2 + m) * 2
                    out_ref[y * TEAM + j, row : row + 2, :] = velocity_ref[c, m, :, lanes]


def scatter(flip, velocity):
    return pl.pallas_call(
        scatter_body,
        out_shape=[jax.ShapeDtypeStruct((4 * TEAM, 16, BLK), F32), jax.ShapeDtypeStruct((8, BLK), F32)],
        in_specs=[pl.BlockSpec(memory_space=pltpu.SMEM)] + vmem(1),
        out_specs=vmem(2),
        compiler_params=LIMIT,
        name="scatter",
    )(flip, velocity)


def nonlinear_core(state, inverse_ref, derivative_ref, forward_ref):
    hi, lo = split(state)
    physical = jnp.dot(inverse_ref[...], jnp.concatenate([hi, lo, hi], axis=0), preferred_element_type=F32)
    field = [physical[:, c * BLK : (c + 1) * BLK] for c in range(3)]
    products = {pair: field[pair[0]] * field[pair[1]] for pair in PAIRS}

    def product(a, b):
        return products[(min(a, b), max(a, b))]

    left = jnp.concatenate([jnp.concatenate([product(a, 0), product(a, 1)], axis=1) for a in range(3)], axis=0)
    left_hi, left_lo = split(left)
    der_hi, der_lo = split(derivative_ref[...])
    planar = jnp.dot(
        jnp.concatenate([left_hi, left_lo], axis=0),
        jnp.concatenate([der_hi, der_lo], axis=1),
        preferred_element_type=F32,
    )
    rows = 3 * POINTS
    planar = planar[:rows, :BLK] + planar[:rows, BLK:] + planar[rows:, :BLK]
    right = jnp.concatenate(
        [jnp.concatenate([planar[a * POINTS : (a + 1) * POINTS], product(a, 2)], axis=0) for a in range(3)], axis=1
    )
    right_hi, right_lo = split(right)
    first = jnp.dot(forward_ref[...], right_hi, preferred_element_type=F32)
    second = jnp.dot(forward_ref[:POINTS, :], right_lo, preferred_element_type=F32)
    return state + (first[:POINTS] + first[POINTS:] + second)


def store_chunks(right_side, out_ref):
    for j in range(TEAM):
        for c in range(3):
            out_ref[j, c * 16 : (c + 1) * 16, :] = right_side[j * 16 : (j + 1) * 16, c * BLK : (c + 1) * BLK]


def first_body(chunks_ref, inverse_ref, derivative_ref, forward_ref, after_ref, out_ref, state_ref):
    for device in range(4 * TEAM):
        y, member = divmod(device, TEAM)
        row = member * 16 + y * 4
        for c in range(3):
            state_ref[row : row + 4, c * BLK : (c + 1) * BLK] = chunks_ref[device, c * 4 : (c + 1) * 4, :]
    store_chunks(nonlinear_core(state_ref[...], inverse_ref, derivative_ref, forward_ref), out_ref)


def later_body(chunks_ref, inverse_ref, derivative_ref, forward_ref, out_ref):
    state = jnp.concatenate(
        [
            jnp.concatenate([chunks_ref[j, c * 16 : (c + 1) * 16, :] for j in range(TEAM)], axis=0)
            for c in range(3)
        ],
        axis=1,
    )
    store_chunks(nonlinear_core(state, inverse_ref, derivative_ref, forward_ref), out_ref)


def nonlinear(chunks, inverse, derivative, forward, after=()):
    first = len(after) > 0
    return pl.pallas_call(
        first_body if first else later_body,
        out_shape=jax.ShapeDtypeStruct((TEAM, VEC, BLK), F32),
        in_specs=vmem(4) + [pl.BlockSpec(memory_space=pl.ANY)] * len(after),
        out_specs=vmem(1)[0],
        scratch_shapes=[pltpu.VMEM((POINTS, 3 * BLK), F32)] if first else [],
        compiler_params=LIMIT,
        name="nonlinear",
    )(chunks, inverse, derivative, forward, *after)


def build_band(near_ref, block_ref, row, centre, acc_ref):
    acc_ref[...] = jnp.zeros_like(acc_ref)
    for slot in range(9):
        offset = near_ref[row * 9 + slot] - centre + HW
        acc_ref[offset] += block_ref[slot]


def fetch_rows(blocks_ref, rows_ref, sem_ref, first, count):
    def copy(i):
        row = jnp.clip(first + i, 0, LOCAL - 1)
        return pltpu.make_async_copy(blocks_ref.at[row], rows_ref.at[i], sem_ref.at[i])

    for i in range(count):
        copy(i).start()
    return copy


def edge_body(near_ref, info_ref, blocks_ref, after_ref, out_ref, rows_ref, sem_ref):
    copy = fetch_rows(blocks_ref, rows_ref, sem_ref, info_ref[1], EDGE)
    for i in range(EDGE):
        row = info_ref[1] + i
        copy(i).wait()
        build_band(near_ref, rows_ref.at[i], row, info_ref[0] + row, out_ref.at[i])


def edge_band(near, info, blocks, after):
    smem = pl.BlockSpec(memory_space=pltpu.SMEM)
    return pl.pallas_call(
        edge_body,
        out_shape=jax.ShapeDtypeStruct((EDGE, BAND, BLK, BLK), F32),
        in_specs=[smem, smem, pl.BlockSpec(memory_space=pltpu.HBM)] + vmem(1),
        out_specs=vmem(1)[0],
        scratch_shapes=[pltpu.VMEM((EDGE, 9, BLK, BLK), F32), pltpu.SemaphoreType.DMA((EDGE,))],
        compiler_params=LARGE,
        cost_estimate=cost(10**6, 6 * 10**6),
        name="edge_band",
    )(near, info, blocks, after)


def store_weights(out_ref, i, offset, block):
    hi, lo = split(block.T)
    out_ref[i, offset * BLK : (offset + 1) * BLK, :BLK] = hi
    out_ref[i, offset * BLK : (offset + 1) * BLK, BLK:] = lo


def weight_body(near_ref, info_ref, blocks_ref, out_ref, done_ref, rows_ref, acc_ref, sem_ref):
    copy = fetch_rows(blocks_ref, rows_ref, sem_ref, info_ref[2], ROWS)
    done_ref[...] = jnp.zeros_like(done_ref)
    for i in range(ROWS):
        row = jnp.clip(info_ref[2] + i, 0, LOCAL - 1)
        copy(i).wait()
        build_band(near_ref, rows_ref.at[i], row, info_ref[0] + row, acc_ref)
        for offset in range(BAND):
            store_weights(out_ref, i, offset, acc_ref[offset])


def weights_of(near, info, blocks):
    smem = pl.BlockSpec(memory_space=pltpu.SMEM)
    return pl.pallas_call(
        weight_body,
        out_shape=[
            jax.ShapeDtypeStruct((ROWS, BAND * BLK, 2 * BLK), BF16),
            jax.ShapeDtypeStruct((8, BLK), F32),
        ],
        in_specs=[smem, smem, pl.BlockSpec(memory_space=pltpu.HBM)],
        out_specs=vmem(2),
        scratch_shapes=[
            pltpu.VMEM((ROWS, 9, BLK, BLK), F32),
            pltpu.VMEM((BAND, BLK, BLK), F32),
            pltpu.SemaphoreType.DMA((ROWS,)),
        ],
        compiler_params=LARGE,
        cost_estimate=cost(10**6, 16 * 10**6),
        name="weights",
    )(near, info, blocks)


def edge_weight_body(edge_ref, out_ref):
    for i in range(EDGE):
        for offset in range(BAND):
            store_weights(out_ref, i, offset, edge_ref[i, offset])


def edge_weights_of(edge):
    return pl.pallas_call(
        edge_weight_body,
        out_shape=jax.ShapeDtypeStruct((EDGE, BAND * BLK, 2 * BLK), BF16),
        in_specs=vmem(1),
        out_specs=vmem(1)[0],
        compiler_params=LIMIT,
        cost_estimate=cost(10**6, 3 * 10**6),
        name="edge_weights",
    )(edge)


def solve_values(place_ref, own_ref, even_swap_ref, odd_swap_ref, weight_ref, edge_ref, coef_ref):
    rank = place_ref[0]
    odd = rank % 2 == 1

    def weight(row):
        if row < EDGE:
            return jnp.where(rank == 0, edge_ref[row], weight_ref[row])
        if row >= EDGE + OWN:
            return jnp.where(rank == 3, edge_ref[row - EDGE - OWN], weight_ref[row])
        return weight_ref[row]

    def window(w):
        if w < OWN:
            return jnp.where(odd, even_swap_ref[w], odd_swap_ref[w])
        if w < 2 * OWN:
            return own_ref[w - OWN]
        return jnp.where(odd, odd_swap_ref[w - 2 * OWN], even_swap_ref[w - 2 * OWN])

    def stacked(x):
        return jnp.concatenate(split(x), axis=0)

    def apply(parts, rows):
        out = {}
        for w in rows:
            lhs = jnp.concatenate([parts[w + o] for o in range(-HW, HW + 1)], axis=1)
            both = jnp.dot(lhs, weight(w - HW), preferred_element_type=F32)
            out[w] = both[:VEC, :BLK] + both[:VEC, BLK:] + both[VEC:, :BLK]
        return out

    one = apply({w: stacked(window(w)) for w in range(WIN)}, range(HW, WIN - HW))
    two = apply({w: stacked(x) for w, x in one.items()}, range(2 * HW, WIN - 2 * HW))
    three = apply({w: stacked(x) for w, x in two.items()}, range(3 * HW, WIN - 3 * HW))
    coef = [coef_ref[:, i : i + 1] for i in range(SWEEPS + 1)]
    return [
        coef[0] * window(w) + coef[1] * one[w] + coef[2] * two[w] + coef[3] * three[w]
        for w in range(OWN, 2 * OWN)
    ]


def solve_body(place_ref, own_ref, even_swap_ref, odd_swap_ref, weight_ref, edge_ref, coef_ref, out_ref):
    for j, x in enumerate(solve_values(place_ref, own_ref, even_swap_ref, odd_swap_ref, weight_ref, edge_ref, coef_ref)):
        out_ref[j] = x
    out_ref[OWN:] = jnp.zeros((TEAM - OWN, VEC, BLK), F32)


def last_body(place_ref, own_ref, even_swap_ref, odd_swap_ref, weight_ref, edge_ref, coef_ref, out_ref):
    for j, x in enumerate(solve_values(place_ref, own_ref, even_swap_ref, odd_swap_ref, weight_ref, edge_ref, coef_ref)):
        for y in range(4):
            for c in range(3):
                out_ref[y, j, c * 4 : (c + 1) * 4, :] = x[c * 16 + y * 4 : c * 16 + y * 4 + 4]
            out_ref[y, j, 12:, :] = jnp.zeros((4, BLK), F32)


def solve(place, own, even_swap, odd_swap, weights, edge, coef, last):
    shape = (4, OWN, 16, BLK) if last else (TEAM, VEC, BLK)
    return pl.pallas_call(
        last_body if last else solve_body,
        out_shape=jax.ShapeDtypeStruct(shape, F32),
        in_specs=[pl.BlockSpec(memory_space=pltpu.SMEM)] + vmem(6),
        out_specs=vmem(1)[0],
        compiler_params=LIMIT,
        name="solve",
    )(place, own, even_swap, odd_swap, weights, edge, coef)


def gather_body(flip_ref, chunks_ref, out_ref):
    flip = flip_ref[0]
    for q in range(4):
        y = q + flip * (3 - 2 * q)
        for j in range(OWN):
            lanes = slice((q * OWN + j) * BLK, (q * OWN + j + 1) * BLK)
            for c in range(3):
                for m in range(2):
                    row = (c * 2 + m) * 2
                    out_ref[c, m, :, lanes] = chunks_ref[y, j, row : row + 2, :]


def gather(flip, chunks):
    return pl.pallas_call(
        gather_body,
        out_shape=jax.ShapeDtypeStruct((3, 2, 2, LOCAL * BLK), F32),
        in_specs=[pl.BlockSpec(memory_space=pltpu.SMEM)] + vmem(1),
        out_specs=vmem(1)[0],
        compiler_params=LIMIT,
        name="gather",
    )(flip, chunks)


def on_device(velocity, blocks, neighbours, element_derivative):
    y, z, xl, xh, co = (lax.axis_index(axis) for axis in AXES)
    part = xh * 2 + co
    q = y + co * (3 - 2 * y)
    flip = co.reshape(1)
    place = q.reshape(1)
    info = jnp.stack([part * LOCAL, jnp.where(q < 2, 0, LOCAL - EDGE), q * OWN - EDGE]).astype(jnp.int32)
    near = neighbours.reshape(-1)
    inverse_np, forward_np = tables()
    inverse, forward = jnp.asarray(inverse_np), jnp.asarray(forward_np)
    coef = lax.dynamic_index_in_dim(jnp.asarray(solve_coefficients()), z * 2 + xl, 0, keepdims=False)
    count = BLK // ELEM
    eye = jnp.eye(count, dtype=F32)
    derivative = (
        eye[None, :, None, :, None] * element_derivative.transpose(0, 2, 1)[:, None, :, None, :]
    ).reshape(2 * BLK, BLK)

    spread, sent = scatter(flip, velocity)
    chunks = lax.all_to_all(spread, ("y", "z", "xl"), 0, 0, tiled=True)
    edge = lax.ppermute(edge_band(near, info, blocks, sent), AXES, seam_pairs())
    weights, built = weights_of(near, info, blocks)
    for step in range(STEPS):
        right_side = nonlinear(chunks, inverse, derivative, forward, (built,) if step == 0 else ())
        own = lax.all_to_all(right_side, ("z", "xl"), 0, 0, tiled=True)
        if step == 0:
            edge_weights = edge_weights_of(edge)
        mine = own[:OWN]
        even_swap = lax.ppermute(mine, AXES, swap_pairs(0))
        odd_swap = lax.ppermute(mine, AXES, swap_pairs(1))
        last = step == STEPS - 1
        chunks = solve(place, own, even_swap, odd_swap, weights, edge_weights, coef, last)
        if not last:
            chunks = lax.all_to_all(chunks, ("z", "xl"), 0, 0, tiled=True)
    return gather(flip, lax.all_to_all(chunks, ("y",), 0, 0, tiled=True))


def solution(mesh):
    fine = Mesh(mesh.devices.reshape(4, 4, 2, 2, 2), AXES)
    field = P(None, ("y", "z", "xl"), None, ("xh", "co"))
    in_specs = (field, P(("xh", "co"), None, None, None), P(("xh", "co"), None), P())
    return jax.shard_map(on_device, mesh=fine, in_specs=in_specs, out_specs=field, check_vma=False)
```

```python
import jax
import jax.numpy as jnp
import numpy as np
from jax import lax
from jax.experimental import pallas as pl
from jax.experimental.pallas import tpu as pltpu
from jax.sharding import Mesh
from jax.sharding import PartitionSpec as P

ELEM = 16
HW = 2
SWEEPS = 3
STEPS = 5
BLK = 128
BAND = 2 * HW + 1

VISCOSITY = 0.1
TIME_STEP = 0.2
HALF_WIDTH = 0.6
SPAN_WAVE = 1.0 / 16.0

MODES = 64
POINTS = 2 * MODES
PAIRS = ((0, 0), (0, 1), (0, 2), (1, 1), (1, 2), (2, 2))
AXES = ("y", "z", "xl", "xh", "co")
TEAM = 8
OWN = 6
VEC = 48
EDGE = 2 * HW
WIN = 3 * OWN
ROWS = OWN + 2 * EDGE
LOCAL = 24

F32 = jnp.float32
BF16 = jnp.bfloat16


def device_of(y, z, xl, xh, co):
    return (((y * 4 + z) * 2 + xl) * 2 + xh) * 2 + co


def team_devices(rank):
    s, q = divmod(rank, 4)
    xh, co = divmod(s, 2)
    y = q if co == 0 else 3 - q
    return [device_of(y, z, xl, xh, co) for z in range(4) for xl in range(2)]


def swap_pairs(first):
    pairs = []
    for rank in range(first, 15, 2):
        for a, b in zip(team_devices(rank), team_devices(rank + 1)):
            pairs += [(a, b), (b, a)]
    return pairs


def seam_pairs():
    pairs = []
    for rank in (3, 7, 11):
        for i, a in enumerate(team_devices(rank)):
            b = team_devices(rank + 1)[i ^ 1 if rank == 7 else i]
            pairs += [(a, b), (b, a)]
    return pairs


def split_np(x):
    hi = x.astype(BF16)
    lo = (x - hi.astype(np.float64)).astype(BF16)
    return hi, lo


def mode_rows():
    modes, parts = [], []
    for member in range(TEAM):
        for y in range(4):
            for m in range(2):
                for r in range(2):
                    modes.append(2 * (y * 8 + member) + m)
                    parts.append(r)
    return np.array(modes), np.array(parts)


def tables():
    modes, parts = mode_rows()
    z = np.arange(POINTS)
    angle = 2.0 * np.pi / POINTS * ((z[:, None] * modes[None, :]) % POINTS)
    cosine, sine = np.cos(angle), np.sin(angle)
    weight = np.where(modes == 0, 1.0, 2.0)
    inverse = np.where(parts == 0, cosine, -sine) * weight
    forward = (np.where(parts == 0, cosine, -sine) / POINTS).T
    wave = modes * SPAN_WAVE
    other = (np.where(parts == 0, -sine, cosine) / POINTS).T
    spanwise = np.where(parts == 0, -wave, wave)[:, None] * other
    both = -TIME_STEP * np.concatenate([forward, spanwise], axis=1)
    ihi, ilo = split_np(inverse)
    fhi, flo = split_np(both)
    return (
        np.concatenate([ihi, ihi, ilo], axis=1),
        np.concatenate([fhi, flo], axis=0),
    )


def solve_coefficients():
    shift = 1.0 + VISCOSITY * (np.arange(MODES) * SPAN_WAVE) ** 2
    sigma = shift / HALF_WIDTH
    old = 1.0 / sigma
    width = SWEEPS + 1
    residual = np.zeros((MODES, width))
    residual[:, 0] = 1.0
    direction = residual / shift[:, None]
    total = np.zeros((MODES, width))
    for _ in range(SWEEPS):
        total = total + direction
        moved = np.concatenate([np.zeros((MODES, 1)), direction[:, :-1]], axis=1)
        residual = residual - (shift[:, None] * direction + moved)
        new = 1.0 / (2.0 * sigma - old)
        direction = (new * old)[:, None] * direction + (2.0 * new / HALF_WIDTH)[:, None] * residual
        old = new
    total = total + direction
    modes, _ = mode_rows()
    out = np.zeros((TEAM, VEC, BLK), np.float32)
    for member in range(TEAM):
        for c in range(3):
            for i in range(16):
                out[member, c * 16 + i, :width] = total[modes[member * 16 + i]]
    return out


def split(x):
    hi = x.astype(BF16)
    return hi, (x - hi.astype(F32)).astype(BF16)


def full(shape):
    return pl.BlockSpec(shape, lambda *_: (0,) * len(shape))


def vmem(n):
    return [pl.BlockSpec(memory_space=pltpu.VMEM)] * n


LIMIT = pltpu.CompilerParams(vmem_limit_bytes=12 * 2**20)
LARGE = pltpu.CompilerParams(vmem_limit_bytes=40 * 2**20)


def cost(flops, transferred):
    return pl.CostEstimate(flops=flops, bytes_accessed=transferred, transcendentals=0)


def scatter_body(flip_ref, velocity_ref, out_ref, done_ref):
    flip = flip_ref[0]
    done_ref[...] = jnp.zeros_like(done_ref)
    out_ref[...] = jnp.zeros_like(out_ref)
    for q in range(4):
        y = q + flip * (3 - 2 * q)
        for j in range(OWN):
            lanes = slice((q * OWN + j) * BLK, (q * OWN + j + 1) * BLK)
            for c in range(3):
                for m in range(2):
                    row = (c * 2 + m) * 2
                    out_ref[y * TEAM + j, row : row + 2, :] = velocity_ref[c, m, :, lanes]


def scatter(flip, velocity):
    return pl.pallas_call(
        scatter_body,
        out_shape=[jax.ShapeDtypeStruct((4 * TEAM, 16, BLK), F32), jax.ShapeDtypeStruct((8, BLK), F32)],
        in_specs=[pl.BlockSpec(memory_space=pltpu.SMEM)] + vmem(1),
        out_specs=vmem(2),
        compiler_params=LIMIT,
        name="scatter",
    )(flip, velocity)


def nonlinear_core(state, inverse_ref, derivative_ref, forward_ref):
    hi, lo = split(state)
    physical = jnp.dot(inverse_ref[...], jnp.concatenate([hi, lo, hi], axis=0), preferred_element_type=F32)
    field = [physical[:, c * BLK : (c + 1) * BLK] for c in range(3)]
    products = {pair: field[pair[0]] * field[pair[1]] for pair in PAIRS}

    def product(a, b):
        return products[(min(a, b), max(a, b))]

    left = jnp.concatenate([jnp.concatenate([product(a, 0), product(a, 1)], axis=1) for a in range(3)], axis=0)
    left_hi, left_lo = split(left)
    der_hi, der_lo = split(derivative_ref[...])
    planar = jnp.dot(
        jnp.concatenate([left_hi, left_lo], axis=0),
        jnp.concatenate([der_hi, der_lo], axis=1),
        preferred_element_type=F32,
    )
    rows = 3 * POINTS
    planar = planar[:rows, :BLK] + planar[:rows, BLK:] + planar[rows:, :BLK]
    right = jnp.concatenate(
        [jnp.concatenate([planar[a * POINTS : (a + 1) * POINTS], product(a, 2)], axis=0) for a in range(3)], axis=1
    )
    right_hi, right_lo = split(right)
    first = jnp.dot(forward_ref[...], right_hi, preferred_element_type=F32)
    second = jnp.dot(forward_ref[:POINTS, :], right_lo, preferred_element_type=F32)
    return state + (first[:POINTS] + first[POINTS:] + second)


def store_chunks(right_side, out_ref):
    for j in range(TEAM):
        for c in range(3):
            out_ref[j, c * 16 : (c + 1) * 16, :] = right_side[j * 16 : (j + 1) * 16, c * BLK : (c + 1) * BLK]


def first_body(chunks_ref, inverse_ref, derivative_ref, forward_ref, after_ref, out_ref, same_ref, state_ref):
    for device in range(4 * TEAM):
        y, member = divmod(device, TEAM)
        row = member * 16 + y * 4
        for c in range(3):
            state_ref[row : row + 4, c * BLK : (c + 1) * BLK] = chunks_ref[device, c * 4 : (c + 1) * 4, :]
    store_chunks(nonlinear_core(state_ref[...], inverse_ref, derivative_ref, forward_ref), out_ref)


def later_body(chunks_ref, inverse_ref, derivative_ref, forward_ref, out_ref):
    state = jnp.concatenate(
        [
            jnp.concatenate([chunks_ref[j, c * 16 : (c + 1) * 16, :] for j in range(TEAM)], axis=0)
            for c in range(3)
        ],
        axis=1,
    )
    store_chunks(nonlinear_core(state, inverse_ref, derivative_ref, forward_ref), out_ref)


def nonlinear(chunks, inverse, derivative, forward, held=None):
    first = held is not None
    out = jax.ShapeDtypeStruct((TEAM, VEC, BLK), F32)
    anywhere = pl.BlockSpec(memory_space=pl.ANY)
    return pl.pallas_call(
        first_body if first else later_body,
        out_shape=[out, jax.ShapeDtypeStruct(held.shape, F32)] if first else out,
        in_specs=vmem(4) + [anywhere] * first,
        out_specs=vmem(1) + [anywhere] if first else vmem(1)[0],
        scratch_shapes=[pltpu.VMEM((POINTS, 3 * BLK), F32)] if first else [],
        input_output_aliases={4: 1} if first else {},
        compiler_params=LIMIT,
        name="nonlinear",
    )(chunks, inverse, derivative, forward, *([held] if first else []))


def build_band(near_ref, block_ref, row, centre, acc_ref):
    acc_ref[...] = jnp.zeros_like(acc_ref)
    for slot in range(9):
        offset = near_ref[slot, row] - centre + HW
        acc_ref[offset] += block_ref[slot]


def fetch_rows(blocks_ref, rows_ref, sem_ref, first, count):
    def copy(i):
        row = jnp.clip(first + i, 0, LOCAL - 1)
        return pltpu.make_async_copy(blocks_ref.at[row], rows_ref.at[i], sem_ref.at[i])

    for i in range(count):
        copy(i).start()
    return copy


def edge_body(near_ref, info_ref, blocks_ref, after_ref, out_ref, rows_ref, sem_ref):
    copy = fetch_rows(blocks_ref, rows_ref, sem_ref, info_ref[1], EDGE)
    for i in range(EDGE):
        row = info_ref[1] + i
        copy(i).wait()
        build_band(near_ref, rows_ref.at[i], row, info_ref[0] + row, out_ref.at[i])


def edge_band(near, info, blocks, after):
    smem = pl.BlockSpec(memory_space=pltpu.SMEM)
    return pl.pallas_call(
        edge_body,
        out_shape=jax.ShapeDtypeStruct((EDGE, BAND, BLK, BLK), F32),
        in_specs=[smem, smem, pl.BlockSpec(memory_space=pltpu.HBM)] + vmem(1),
        out_specs=vmem(1)[0],
        scratch_shapes=[pltpu.VMEM((EDGE, 9, BLK, BLK), F32), pltpu.SemaphoreType.DMA((EDGE,))],
        compiler_params=LARGE,
        cost_estimate=cost(10**6, 6 * 10**6),
        name="edge_band",
    )(near, info, blocks, after)


def store_weights(out_ref, i, offset, block):
    hi, lo = split(block.T)
    out_ref[i, offset * BLK : (offset + 1) * BLK, :BLK] = hi
    out_ref[i, offset * BLK : (offset + 1) * BLK, BLK:] = lo


def weight_body(near_ref, info_ref, blocks_ref, out_ref, done_ref, rows_ref, acc_ref, sem_ref):
    copy = fetch_rows(blocks_ref, rows_ref, sem_ref, info_ref[2], ROWS)
    done_ref[...] = jnp.zeros_like(done_ref)
    for i in range(ROWS):
        row = jnp.clip(info_ref[2] + i, 0, LOCAL - 1)
        copy(i).wait()
        build_band(near_ref, rows_ref.at[i], row, info_ref[0] + row, acc_ref)
        for offset in range(BAND):
            store_weights(out_ref, i, offset, acc_ref[offset])


def weights_of(near, info, blocks):
    smem = pl.BlockSpec(memory_space=pltpu.SMEM)
    return pl.pallas_call(
        weight_body,
        out_shape=[
            jax.ShapeDtypeStruct((ROWS, BAND * BLK, 2 * BLK), BF16),
            jax.ShapeDtypeStruct((8, BLK), F32),
        ],
        in_specs=[smem, smem, pl.BlockSpec(memory_space=pltpu.HBM)],
        out_specs=vmem(2),
        scratch_shapes=[
            pltpu.VMEM((ROWS, 9, BLK, BLK), F32),
            pltpu.VMEM((BAND, BLK, BLK), F32),
            pltpu.SemaphoreType.DMA((ROWS,)),
        ],
        compiler_params=LARGE,
        cost_estimate=cost(10**6, 16 * 10**6),
        name="weights",
    )(near, info, blocks)


def edge_weight_body(edge_ref, out_ref):
    for i in range(EDGE):
        for offset in range(BAND):
            store_weights(out_ref, i, offset, edge_ref[i, offset])


def edge_weights_of(edge):
    return pl.pallas_call(
        edge_weight_body,
        out_shape=jax.ShapeDtypeStruct((EDGE, BAND * BLK, 2 * BLK), BF16),
        in_specs=vmem(1),
        out_specs=vmem(1)[0],
        compiler_params=LIMIT,
        cost_estimate=cost(10**6, 3 * 10**6),
        name="edge_weights",
    )(edge)


def solve_values(place_ref, own_ref, even_swap_ref, odd_swap_ref, weight_ref, edge_ref, coef_ref):
    rank = place_ref[0]
    odd = rank % 2 == 1

    def weight(row):
        if row < EDGE:
            return jnp.where(rank == 0, edge_ref[row], weight_ref[row])
        if row >= EDGE + OWN:
            return jnp.where(rank == 3, edge_ref[row - EDGE - OWN], weight_ref[row])
        return weight_ref[row]

    def window(w):
        if w < OWN:
            return jnp.where(odd, even_swap_ref[w], odd_swap_ref[w])
        if w < 2 * OWN:
            return own_ref[w - OWN]
        return jnp.where(odd, odd_swap_ref[w - 2 * OWN], even_swap_ref[w - 2 * OWN])

    def stacked(x):
        return jnp.concatenate(split(x), axis=0)

    def apply(parts, rows):
        out = {}
        for w in rows:
            lhs = jnp.concatenate([parts[w + o] for o in range(-HW, HW + 1)], axis=1)
            both = jnp.dot(lhs, weight(w - HW), preferred_element_type=F32)
            out[w] = both[:VEC, :BLK] + both[:VEC, BLK:] + both[VEC:, :BLK]
        return out

    one = apply({w: stacked(window(w)) for w in range(WIN)}, range(HW, WIN - HW))
    two = apply({w: stacked(x) for w, x in one.items()}, range(2 * HW, WIN - 2 * HW))
    three = apply({w: stacked(x) for w, x in two.items()}, range(3 * HW, WIN - 3 * HW))
    coef = [coef_ref[:, i : i + 1] for i in range(SWEEPS + 1)]
    return [
        coef[0] * window(w) + coef[1] * one[w] + coef[2] * two[w] + coef[3] * three[w]
        for w in range(OWN, 2 * OWN)
    ]


def solve_body(place_ref, own_ref, even_swap_ref, odd_swap_ref, weight_ref, edge_ref, coef_ref, out_ref):
    for j, x in enumerate(solve_values(place_ref, own_ref, even_swap_ref, odd_swap_ref, weight_ref, edge_ref, coef_ref)):
        out_ref[j] = x
    out_ref[OWN:] = jnp.zeros((TEAM - OWN, VEC, BLK), F32)


def last_body(place_ref, own_ref, even_swap_ref, odd_swap_ref, weight_ref, edge_ref, coef_ref, out_ref):
    for j, x in enumerate(solve_values(place_ref, own_ref, even_swap_ref, odd_swap_ref, weight_ref, edge_ref, coef_ref)):
        for y in range(4):
            for c in range(3):
                out_ref[y, j, c * 4 : (c + 1) * 4, :] = x[c * 16 + y * 4 : c * 16 + y * 4 + 4]
            out_ref[y, j, 12:, :] = jnp.zeros((4, BLK), F32)


def solve(place, own, even_swap, odd_swap, weights, edge, coef, last):
    shape = (4, OWN, 16, BLK) if last else (TEAM, VEC, BLK)
    return pl.pallas_call(
        last_body if last else solve_body,
        out_shape=jax.ShapeDtypeStruct(shape, F32),
        in_specs=[pl.BlockSpec(memory_space=pltpu.SMEM)] + vmem(6),
        out_specs=vmem(1)[0],
        compiler_params=LIMIT,
        name="solve",
    )(place, own, even_swap, odd_swap, weights, edge, coef)


def gather_body(flip_ref, chunks_ref, out_ref):
    flip = flip_ref[0]
    for q in range(4):
        y = q + flip * (3 - 2 * q)
        for j in range(OWN):
            lanes = slice((q * OWN + j) * BLK, (q * OWN + j + 1) * BLK)
            for c in range(3):
                for m in range(2):
                    row = (c * 2 + m) * 2
                    out_ref[c, m, :, lanes] = chunks_ref[y, j, row : row + 2, :]


def gather(flip, chunks):
    return pl.pallas_call(
        gather_body,
        out_shape=jax.ShapeDtypeStruct((3, 2, 2, LOCAL * BLK), F32),
        in_specs=[pl.BlockSpec(memory_space=pltpu.SMEM)] + vmem(1),
        out_specs=vmem(1)[0],
        compiler_params=LIMIT,
        name="gather",
    )(flip, chunks)


def on_device(velocity, blocks, neighbours, element_derivative):
    y, z, xl, xh, co = (lax.axis_index(axis) for axis in AXES)
    part = xh * 2 + co
    q = y + co * (3 - 2 * y)
    flip = co.reshape(1)
    place = q.reshape(1)
    info = jnp.stack([part * LOCAL, jnp.where(q < 2, 0, LOCAL - EDGE), q * OWN - EDGE]).astype(jnp.int32)
    inverse_np, forward_np = tables()
    inverse, forward = jnp.asarray(inverse_np), jnp.asarray(forward_np)
    coef = lax.dynamic_index_in_dim(jnp.asarray(solve_coefficients()), z * 2 + xl, 0, keepdims=False)
    count = BLK // ELEM
    eye = jnp.eye(count, dtype=F32)
    derivative = (
        eye[None, :, None, :, None] * element_derivative.transpose(0, 2, 1)[:, None, :, None, :]
    ).reshape(2 * BLK, BLK)

    spread, sent = scatter(flip, velocity)
    chunks = lax.all_to_all(spread, ("y", "z", "xl"), 0, 0, tiled=True)
    ends = edge_band(neighbours.T, info, blocks, sent)
    weights, built = weights_of(neighbours.T, info, blocks)
    for step in range(STEPS):
        if step == 0:
            right_side, ends = nonlinear(chunks, inverse, derivative, forward, ends)
            edge = lax.ppermute(ends, AXES, seam_pairs())
        else:
            right_side = nonlinear(chunks, inverse, derivative, forward)
        own = lax.all_to_all(right_side, ("z", "xl"), 0, 0, tiled=True)
        if step == 0:
            edge_weights = edge_weights_of(edge)
        mine = own[:OWN]
        even_swap = lax.ppermute(mine, AXES, swap_pairs(0))
        odd_swap = lax.ppermute(mine, AXES, swap_pairs(1))
        last = step == STEPS - 1
        chunks = solve(place, own, even_swap, odd_swap, weights, edge_weights, coef, last)
        if not last:
            chunks = lax.all_to_all(chunks, ("z", "xl"), 0, 0, tiled=True)
    return gather(flip, lax.all_to_all(chunks, ("y",), 0, 0, tiled=True))


def solution(mesh):
    fine = Mesh(mesh.devices.reshape(4, 4, 2, 2, 2), AXES)
    field = P(None, ("y", "z", "xl"), None, ("xh", "co"))
    in_specs = (field, P(("xh", "co"), None, None, None), P(("xh", "co"), None), P())
    return jax.shard_map(on_device, mesh=fine, in_specs=in_specs, out_specs=field, check_vma=False)
```

```python
import jax
import jax.numpy as jnp
import numpy as np
from jax import lax
from jax.experimental import pallas as pl
from jax.experimental.pallas import tpu as pltpu
from jax.sharding import Mesh
from jax.sharding import PartitionSpec as P

ELEM = 16
HW = 2
SWEEPS = 3
STEPS = 5
BLK = 128
BAND = 2 * HW + 1

VISCOSITY = 0.1
TIME_STEP = 0.2
HALF_WIDTH = 0.6
SPAN_WAVE = 1.0 / 16.0

MODES = 64
POINTS = 2 * MODES
PAIRS = ((0, 0), (0, 1), (0, 2), (1, 1), (1, 2), (2, 2))
AXES = ("y", "z", "xl", "xh", "co")
TEAM = 8
OWN = 6
VEC = 48
EDGE = 2 * HW
WIN = 3 * OWN
ROWS = OWN + 2 * EDGE
LOCAL = 24

F32 = jnp.float32
BF16 = jnp.bfloat16


def device_of(y, z, xl, xh, co):
    return (((y * 4 + z) * 2 + xl) * 2 + xh) * 2 + co


def team_devices(rank):
    s, q = divmod(rank, 4)
    xh, co = divmod(s, 2)
    y = q if co == 0 else 3 - q
    return [device_of(y, z, xl, xh, co) for z in range(4) for xl in range(2)]


def swap_pairs(first):
    pairs = []
    for rank in range(first, 15, 2):
        for a, b in zip(team_devices(rank), team_devices(rank + 1)):
            pairs += [(a, b), (b, a)]
    return pairs


def seam_pairs():
    pairs = []
    for rank in (3, 7, 11):
        for i, a in enumerate(team_devices(rank)):
            b = team_devices(rank + 1)[i ^ 1 if rank == 7 else i]
            pairs += [(a, b), (b, a)]
    return pairs


def split_np(x):
    hi = x.astype(BF16)
    lo = (x - hi.astype(np.float64)).astype(BF16)
    return hi, lo


def mode_rows():
    modes, parts = [], []
    for member in range(TEAM):
        for y in range(4):
            for m in range(2):
                for r in range(2):
                    modes.append(2 * (y * 8 + member) + m)
                    parts.append(r)
    return np.array(modes), np.array(parts)


def tables():
    modes, parts = mode_rows()
    z = np.arange(POINTS)
    angle = 2.0 * np.pi / POINTS * ((z[:, None] * modes[None, :]) % POINTS)
    cosine, sine = np.cos(angle), np.sin(angle)
    weight = np.where(modes == 0, 1.0, 2.0)
    inverse = np.where(parts == 0, cosine, -sine) * weight
    forward = (np.where(parts == 0, cosine, -sine) / POINTS).T
    wave = modes * SPAN_WAVE
    other = (np.where(parts == 0, -sine, cosine) / POINTS).T
    spanwise = np.where(parts == 0, -wave, wave)[:, None] * other
    both = -TIME_STEP * np.concatenate([forward, spanwise], axis=1)
    ihi, ilo = split_np(inverse)
    fhi, flo = split_np(both)
    return (
        np.concatenate([ihi, ihi, ilo], axis=1),
        np.concatenate([fhi, flo], axis=0),
    )


def solve_coefficients():
    shift = 1.0 + VISCOSITY * (np.arange(MODES) * SPAN_WAVE) ** 2
    sigma = shift / HALF_WIDTH
    old = 1.0 / sigma
    width = SWEEPS + 1
    residual = np.zeros((MODES, width))
    residual[:, 0] = 1.0
    direction = residual / shift[:, None]
    total = np.zeros((MODES, width))
    for _ in range(SWEEPS):
        total = total + direction
        moved = np.concatenate([np.zeros((MODES, 1)), direction[:, :-1]], axis=1)
        residual = residual - (shift[:, None] * direction + moved)
        new = 1.0 / (2.0 * sigma - old)
        direction = (new * old)[:, None] * direction + (2.0 * new / HALF_WIDTH)[:, None] * residual
        old = new
    total = total + direction
    modes, _ = mode_rows()
    out = np.zeros((TEAM, VEC, BLK), np.float32)
    for member in range(TEAM):
        for c in range(3):
            for i in range(16):
                out[member, c * 16 + i, :width] = total[modes[member * 16 + i]]
    return out


def split(x):
    hi = x.astype(BF16)
    return hi, (x - hi.astype(F32)).astype(BF16)


def full(shape):
    return pl.BlockSpec(shape, lambda *_: (0,) * len(shape))


def vmem(n):
    return [pl.BlockSpec(memory_space=pltpu.VMEM)] * n


LIMIT = pltpu.CompilerParams(vmem_limit_bytes=12 * 2**20)
MIDDLE = pltpu.CompilerParams(vmem_limit_bytes=16 * 2**20)
LARGE = pltpu.CompilerParams(vmem_limit_bytes=40 * 2**20)


def cost(flops, transferred):
    return pl.CostEstimate(flops=flops, bytes_accessed=transferred, transcendentals=0)


def scatter_body(flip_ref, velocity_ref, out_ref, done_ref):
    flip = flip_ref[0]
    done_ref[...] = jnp.zeros_like(done_ref)
    out_ref[...] = jnp.zeros_like(out_ref)
    for q in range(4):
        y = q + flip * (3 - 2 * q)
        for j in range(OWN):
            lanes = slice((q * OWN + j) * BLK, (q * OWN + j + 1) * BLK)
            for c in range(3):
                for m in range(2):
                    row = (c * 2 + m) * 2
                    out_ref[y * TEAM + j, row : row + 2, :] = velocity_ref[c, m, :, lanes]


def scatter(flip, velocity):
    return pl.pallas_call(
        scatter_body,
        out_shape=[jax.ShapeDtypeStruct((4 * TEAM, 16, BLK), F32), jax.ShapeDtypeStruct((8, BLK), F32)],
        in_specs=[pl.BlockSpec(memory_space=pltpu.SMEM)] + vmem(1),
        out_specs=vmem(2),
        compiler_params=LIMIT,
        name="scatter",
    )(flip, velocity)


def nonlinear_core(state, inverse_ref, derivative_ref, forward_ref):
    hi, lo = split(state)
    physical = jnp.dot(inverse_ref[...], jnp.concatenate([hi, lo, hi], axis=0), preferred_element_type=F32)
    field = [physical[:, c * BLK : (c + 1) * BLK] for c in range(3)]
    products = {pair: field[pair[0]] * field[pair[1]] for pair in PAIRS}

    def product(a, b):
        return products[(min(a, b), max(a, b))]

    left = jnp.concatenate([jnp.concatenate([product(a, 0), product(a, 1)], axis=1) for a in range(3)], axis=0)
    left_hi, left_lo = split(left)
    der_hi, der_lo = split(derivative_ref[...])
    planar = jnp.dot(
        jnp.concatenate([left_hi, left_lo], axis=0),
        jnp.concatenate([der_hi, der_lo], axis=1),
        preferred_element_type=F32,
    )
    rows = 3 * POINTS
    planar = planar[:rows, :BLK] + planar[:rows, BLK:] + planar[rows:, :BLK]
    right = jnp.concatenate(
        [jnp.concatenate([planar[a * POINTS : (a + 1) * POINTS], product(a, 2)], axis=0) for a in range(3)], axis=1
    )
    right_hi, right_lo = split(right)
    first = jnp.dot(forward_ref[...], right_hi, preferred_element_type=F32)
    second = jnp.dot(forward_ref[:POINTS, :], right_lo, preferred_element_type=F32)
    return state + (first[:POINTS] + first[POINTS:] + second)


def store_chunks(right_side, out_ref):
    for j in range(TEAM):
        for c in range(3):
            out_ref[j, c * 16 : (c + 1) * 16, :] = right_side[j * 16 : (j + 1) * 16, c * BLK : (c + 1) * BLK]


def first_body(chunks_ref, inverse_ref, derivative_ref, forward_ref, after_ref, out_ref, same_ref, state_ref):
    for device in range(4 * TEAM):
        y, member = divmod(device, TEAM)
        row = member * 16 + y * 4
        for c in range(3):
            state_ref[row : row + 4, c * BLK : (c + 1) * BLK] = chunks_ref[device, c * 4 : (c + 1) * 4, :]
    store_chunks(nonlinear_core(state_ref[...], inverse_ref, derivative_ref, forward_ref), out_ref)


def later_body(chunks_ref, inverse_ref, derivative_ref, forward_ref, out_ref):
    state = jnp.concatenate(
        [
            jnp.concatenate([chunks_ref[j, c * 16 : (c + 1) * 16, :] for j in range(TEAM)], axis=0)
            for c in range(3)
        ],
        axis=1,
    )
    store_chunks(nonlinear_core(state, inverse_ref, derivative_ref, forward_ref), out_ref)


def nonlinear(chunks, inverse, derivative, forward, held=None):
    first = held is not None
    out = jax.ShapeDtypeStruct((TEAM, VEC, BLK), F32)
    anywhere = pl.BlockSpec(memory_space=pl.ANY)
    return pl.pallas_call(
        first_body if first else later_body,
        out_shape=[out, jax.ShapeDtypeStruct(held.shape, F32)] if first else out,
        in_specs=vmem(4) + [anywhere] * first,
        out_specs=vmem(1) + [anywhere] if first else vmem(1)[0],
        scratch_shapes=[pltpu.VMEM((POINTS, 3 * BLK), F32)] if first else [],
        input_output_aliases={4: 1} if first else {},
        compiler_params=LIMIT,
        name="nonlinear",
    )(chunks, inverse, derivative, forward, *([held] if first else []))


def build_band(near_ref, block_ref, row, centre, acc_ref):
    acc_ref[...] = jnp.zeros_like(acc_ref)
    for slot in range(9):
        offset = near_ref[slot, row] - centre + HW
        acc_ref[offset] += block_ref[slot]


def fetch_rows(blocks_ref, rows_ref, sem_ref, first, count):
    def copy(i):
        row = jnp.clip(first + i, 0, LOCAL - 1)
        return pltpu.make_async_copy(blocks_ref.at[row], rows_ref.at[i], sem_ref.at[i])

    for i in range(count):
        copy(i).start()
    return copy


def edge_body(near_ref, info_ref, blocks_ref, after_ref, out_ref, rows_ref, sem_ref):
    copy = fetch_rows(blocks_ref, rows_ref, sem_ref, info_ref[1], EDGE)
    for i in range(EDGE):
        row = info_ref[1] + i
        copy(i).wait()
        build_band(near_ref, rows_ref.at[i], row, info_ref[0] + row, out_ref.at[i])


def edge_band(near, info, blocks, after):
    smem = pl.BlockSpec(memory_space=pltpu.SMEM)
    return pl.pallas_call(
        edge_body,
        out_shape=jax.ShapeDtypeStruct((EDGE, BAND, BLK, BLK), F32),
        in_specs=[smem, smem, pl.BlockSpec(memory_space=pltpu.HBM)] + vmem(1),
        out_specs=vmem(1)[0],
        scratch_shapes=[pltpu.VMEM((EDGE, 9, BLK, BLK), F32), pltpu.SemaphoreType.DMA((EDGE,))],
        compiler_params=LARGE,
        cost_estimate=cost(10**6, 6 * 10**6),
        name="edge_band",
    )(near, info, blocks, after)


def store_weights(out_ref, i, offset, block):
    hi, lo = split(block.T)
    out_ref[i, offset * BLK : (offset + 1) * BLK, :BLK] = hi
    out_ref[i, offset * BLK : (offset + 1) * BLK, BLK:] = lo


def weight_body(near_ref, info_ref, blocks_ref, out_ref, done_ref, rows_ref, acc_ref, sem_ref):
    copy = fetch_rows(blocks_ref, rows_ref, sem_ref, info_ref[2], ROWS)
    done_ref[...] = jnp.zeros_like(done_ref)
    for i in range(ROWS):
        row = jnp.clip(info_ref[2] + i, 0, LOCAL - 1)
        copy(i).wait()
        build_band(near_ref, rows_ref.at[i], row, info_ref[0] + row, acc_ref)
        for offset in range(BAND):
            store_weights(out_ref, i, offset, acc_ref[offset])


def weights_of(near, info, blocks):
    smem = pl.BlockSpec(memory_space=pltpu.SMEM)
    return pl.pallas_call(
        weight_body,
        out_shape=[
            jax.ShapeDtypeStruct((ROWS, BAND * BLK, 2 * BLK), BF16),
            jax.ShapeDtypeStruct((8, BLK), F32),
        ],
        in_specs=[smem, smem, pl.BlockSpec(memory_space=pltpu.HBM)],
        out_specs=vmem(2),
        scratch_shapes=[
            pltpu.VMEM((ROWS, 9, BLK, BLK), F32),
            pltpu.VMEM((BAND, BLK, BLK), F32),
            pltpu.SemaphoreType.DMA((ROWS,)),
        ],
        compiler_params=MIDDLE,
        cost_estimate=cost(10**6, 16 * 10**6),
        name="weights",
    )(near, info, blocks)


def edge_weight_body(edge_ref, out_ref):
    for i in range(EDGE):
        for offset in range(BAND):
            store_weights(out_ref, i, offset, edge_ref[i, offset])


def edge_weights_of(edge):
    return pl.pallas_call(
        edge_weight_body,
        out_shape=jax.ShapeDtypeStruct((EDGE, BAND * BLK, 2 * BLK), BF16),
        in_specs=vmem(1),
        out_specs=vmem(1)[0],
        compiler_params=LIMIT,
        cost_estimate=cost(10**6, 3 * 10**6),
        name="edge_weights",
    )(edge)


def solve_values(place_ref, own_ref, even_swap_ref, odd_swap_ref, weight_ref, edge_ref, coef_ref):
    rank = place_ref[0]
    odd = rank % 2 == 1

    def weight(row):
        if row < EDGE:
            return jnp.where(rank == 0, edge_ref[row], weight_ref[row])
        if row >= EDGE + OWN:
            return jnp.where(rank == 3, edge_ref[row - EDGE - OWN], weight_ref[row])
        return weight_ref[row]

    def window(w):
        if w < OWN:
            return jnp.where(odd, even_swap_ref[w], odd_swap_ref[w])
        if w < 2 * OWN:
            return own_ref[w - OWN]
        return jnp.where(odd, odd_swap_ref[w - 2 * OWN], even_swap_ref[w - 2 * OWN])

    def stacked(x):
        return jnp.concatenate(split(x), axis=0)

    def apply(parts, rows):
        out = {}
        for w in rows:
            lhs = jnp.concatenate([parts[w + o] for o in range(-HW, HW + 1)], axis=1)
            both = jnp.dot(lhs, weight(w - HW), preferred_element_type=F32)
            out[w] = both[:VEC, :BLK] + both[:VEC, BLK:] + both[VEC:, :BLK]
        return out

    one = apply({w: stacked(window(w)) for w in range(WIN)}, range(HW, WIN - HW))
    two = apply({w: stacked(x) for w, x in one.items()}, range(2 * HW, WIN - 2 * HW))
    three = apply({w: stacked(x) for w, x in two.items()}, range(3 * HW, WIN - 3 * HW))
    coef = [coef_ref[:, i : i + 1] for i in range(SWEEPS + 1)]
    return [
        coef[0] * window(w) + coef[1] * one[w] + coef[2] * two[w] + coef[3] * three[w]
        for w in range(OWN, 2 * OWN)
    ]


def solve_body(place_ref, own_ref, even_swap_ref, odd_swap_ref, weight_ref, edge_ref, coef_ref, out_ref):
    for j, x in enumerate(solve_values(place_ref, own_ref, even_swap_ref, odd_swap_ref, weight_ref, edge_ref, coef_ref)):
        out_ref[j] = x
    out_ref[OWN:] = jnp.zeros((TEAM - OWN, VEC, BLK), F32)


def last_body(place_ref, own_ref, even_swap_ref, odd_swap_ref, weight_ref, edge_ref, coef_ref, out_ref):
    for j, x in enumerate(solve_values(place_ref, own_ref, even_swap_ref, odd_swap_ref, weight_ref, edge_ref, coef_ref)):
        for y in range(4):
            for c in range(3):
                out_ref[y, j, c * 4 : (c + 1) * 4, :] = x[c * 16 + y * 4 : c * 16 + y * 4 + 4]
            out_ref[y, j, 12:, :] = jnp.zeros((4, BLK), F32)


def solve(place, own, even_swap, odd_swap, weights, edge, coef, last):
    shape = (4, OWN, 16, BLK) if last else (TEAM, VEC, BLK)
    return pl.pallas_call(
        last_body if last else solve_body,
        out_shape=jax.ShapeDtypeStruct(shape, F32),
        in_specs=[pl.BlockSpec(memory_space=pltpu.SMEM)] + vmem(6),
        out_specs=vmem(1)[0],
        compiler_params=LIMIT,
        name="solve",
    )(place, own, even_swap, odd_swap, weights, edge, coef)


def gather_body(flip_ref, chunks_ref, out_ref):
    flip = flip_ref[0]
    for q in range(4):
        y = q + flip * (3 - 2 * q)
        for j in range(OWN):
            lanes = slice((q * OWN + j) * BLK, (q * OWN + j + 1) * BLK)
            for c in range(3):
                for m in range(2):
                    row = (c * 2 + m) * 2
                    out_ref[c, m, :, lanes] = chunks_ref[y, j, row : row + 2, :]


def gather(flip, chunks):
    return pl.pallas_call(
        gather_body,
        out_shape=jax.ShapeDtypeStruct((3, 2, 2, LOCAL * BLK), F32),
        in_specs=[pl.BlockSpec(memory_space=pltpu.SMEM)] + vmem(1),
        out_specs=vmem(1)[0],
        compiler_params=LIMIT,
        name="gather",
    )(flip, chunks)


def on_device(velocity, blocks, neighbours, element_derivative):
    y, z, xl, xh, co = (lax.axis_index(axis) for axis in AXES)
    part = xh * 2 + co
    q = y + co * (3 - 2 * y)
    flip = co.reshape(1)
    place = q.reshape(1)
    info = jnp.stack([part * LOCAL, jnp.where(q < 2, 0, LOCAL - EDGE), q * OWN - EDGE]).astype(jnp.int32)
    inverse_np, forward_np = tables()
    inverse, forward = jnp.asarray(inverse_np), jnp.asarray(forward_np)
    coef = lax.dynamic_index_in_dim(jnp.asarray(solve_coefficients()), z * 2 + xl, 0, keepdims=False)
    count = BLK // ELEM
    eye = jnp.eye(count, dtype=F32)
    derivative = (
        eye[None, :, None, :, None] * element_derivative.transpose(0, 2, 1)[:, None, :, None, :]
    ).reshape(2 * BLK, BLK)

    spread, sent = scatter(flip, velocity)
    chunks = lax.all_to_all(spread, ("y", "z", "xl"), 0, 0, tiled=True)
    ends = edge_band(neighbours.T, info, blocks, sent)
    weights, built = weights_of(neighbours.T, info, blocks)
    for step in range(STEPS):
        if step == 0:
            right_side, ends = nonlinear(chunks, inverse, derivative, forward, ends)
            edge = lax.ppermute(ends, AXES, seam_pairs())
        else:
            right_side = nonlinear(chunks, inverse, derivative, forward)
        own = lax.all_to_all(right_side, ("z", "xl"), 0, 0, tiled=True)
        if step == 0:
            edge_weights = edge_weights_of(edge)
        mine = own[:OWN]
        even_swap = lax.ppermute(mine, AXES, swap_pairs(0))
        odd_swap = lax.ppermute(mine, AXES, swap_pairs(1))
        last = step == STEPS - 1
        chunks = solve(place, own, even_swap, odd_swap, weights, edge_weights, coef, last)
        if not last:
            chunks = lax.all_to_all(chunks, ("z", "xl"), 0, 0, tiled=True)
    return gather(flip, lax.all_to_all(chunks, ("y",), 0, 0, tiled=True))


def solution(mesh):
    fine = Mesh(mesh.devices.reshape(4, 4, 2, 2, 2), AXES)
    field = P(None, ("y", "z", "xl"), None, ("xh", "co"))
    in_specs = (field, P(("xh", "co"), None, None, None), P(("xh", "co"), None), P())
    return jax.shard_map(on_device, mesh=fine, in_specs=in_specs, out_specs=field, check_vma=False)
```
